32 devices in a mesh: expert: 2 (over x), seq: 4 (over z), fsdp: 4 (over y, core).
Axes of the slice: x: 2, y: 2, z: 4, core: 2. Of those that a mesh axis runs over, the one named last changes fastest.
Arguments:
- queries: bfloat16 [16384, 5120], P(('expert', 'seq', 'fsdp')), parts along dimension 0, may hold values from -100 to 100
- keys: bfloat16 [16384, 5120], P(('expert', 'seq', 'fsdp')), parts along dimension 0, may hold values from -100 to 100
- values: bfloat16 [16384, 5120], P(('expert', 'seq', 'fsdp')), parts along dimension 0, may hold values from -6 to 6
- query_gain: float32 [10240], P('expert'), parts along dimension 0, may hold values from 1 to 3
- key_gain: float32 [10240], P('expert'), parts along dimension 0, may hold values from 1 to 3
- timestep: int32 [2], P('expert'), parts along dimension 0, may hold values from 0 to 999, as said below
- gate_base: float32 [10240], P('expert'), parts along dimension 0, may hold values from -3 to 3
- time_weight: float32 [512, 5120], P('expert'), parts along dimension 0, may hold values from -0.375 to 0.375
Outputs:
- attended: bfloat16 [16384, 5120], P(('expert', 'seq', 'fsdp')), parts along dimension 0
The draws below stay inside these ranges and needn't reach their ends.
There are 2 independent parts, one for each index of `expert`. The reference program is written for one: setup_inputs(seed, part) draws one part's arguments, and reference() takes and returns one part's arrays. A program takes and returns all parts, laid end to end along the dimension named above; each array names one. Nothing has to cross between parts.
Inputs may be any that keep to these rules, and one draw needn't show every extreme that they name: Part 0 is the high-noise group, with a timestep from 875 to 999; part 1 the low-noise group, with one from 0 to 874.
All inputs are finite; a program needn't handle non-finite values.
Results may differ from the reference program's by a relative error of at most 0.012.
The reference program's roundings to bfloat16 on the way count: a program that leaves them out, or rounds other values in their place, can miss the bound.
Values may be sent and summed in bfloat16 or wider, within the bound.
A program may use at most 384 MiB of HBM per device.

```python
import math
import jax
import jax.numpy as jnp
from jax import lax

D = 5120
HEADS = 40
HEAD_DIM = 128
FREQ = 256
HGT = 32
WID = 32
NSTEPS = 1000
BOUNDARY = 875
LENGTH = 8192


def noise_field(key, salt, row_total):
    drawn = jax.random.normal(jax.random.fold_in(key, salt), (row_total, D), jnp.float32)
    return jnp.clip(drawn, -6.0, 6.0)


def draw_queries(key, part):
    tensor = noise_field(key, 21, LENGTH)
    return tensor.astype(jnp.bfloat16)


def draw_keys(key, part):
    tensor = noise_field(key, 31, LENGTH)
    return tensor.astype(jnp.bfloat16)


def draw_timestep(key, part):
    upper_draw = jax.random.randint(jax.random.fold_in(key, 41), (1,), BOUNDARY, NSTEPS)
    lower_draw = jax.random.randint(jax.random.fold_in(key, 42), (1,), 0, BOUNDARY)
    return jnp.where(part == 0, upper_draw, lower_draw).astype(jnp.int32)


def block_levels(own_key, extent, cuts, smallest, largest):
    level = 1.0
    for dim, parts in cuts:
        steps = jax.random.uniform(jax.random.fold_in(jax.random.fold_in(own_key, 6), dim), (parts,), jnp.float32, smallest / len(cuts), largest / len(cuts))
        level = level * jnp.repeat(jnp.exp(steps), extent[dim] // parts).reshape((-1,) + (1,) * (len(extent) - 1 - dim))
    return level


def normal_values(own_key, extent, spread, bound, cuts=(), held_as=jnp.bfloat16):
    factor_of = block_levels(own_key, extent, cuts, -0.22, 0.18) if cuts else 1.0
    values = jax.random.normal(own_key, extent, jnp.float32) * spread * factor_of
    return jnp.minimum(jnp.maximum(values, -bound), bound).astype(held_as)


def setup_inputs(seed: int = 0, part: int = 0) -> dict:
    key_list = jax.random.split(jax.random.key(seed), 9)
    own_keys = jax.random.split(jax.random.fold_in(key_list[8], part), 9)
    queries = draw_queries(jax.random.fold_in(jax.random.fold_in(key_list[8], part), 71), part)
    keys = draw_keys(jax.random.fold_in(jax.random.fold_in(key_list[8], part), 71), part)
    values = normal_values(own_keys[2], (LENGTH, D), 1.0, 6.0, ((0, 16),))
    query_gain = jnp.clip(jax.random.uniform(own_keys[3], (D,), jnp.float32, 1.0, 3.0), 1.0, 3.0)
    key_gain = jnp.clip(jax.random.uniform(own_keys[4], (D,), jnp.float32, 1.0, 3.0), 1.0, 3.0)
    timestep = draw_timestep(jax.random.fold_in(jax.random.fold_in(key_list[8], part), 71), part)
    gate_base = normal_values(own_keys[6], (D,), 0.5, 3.0, (), jnp.float32)
    time_weight = normal_values(own_keys[7], (FREQ, D), FREQ ** -0.5, 0.375, (), jnp.float32)
    return {"queries": queries, "keys": keys, "values": values, "query_gain": query_gain, "key_gain": key_gain, "timestep": timestep, "gate_base": gate_base, "time_weight": time_weight}


EPSILON = 1e-06

def rms_normed(tensor, gain_vector):
    mean_square = lax.optimization_barrier(jnp.mean(tensor * tensor, axis=-1, keepdims=True))
    return tensor * lax.rsqrt(mean_square + EPSILON) * gain_vector

def rotate_pairs(tensor, positions):
    half_dim = HEAD_DIM // 2
    sixth = HEAD_DIM // 6
    frame_pairs = (HEAD_DIM - 4 * sixth) // 2
    pair_index = jnp.arange(half_dim, dtype=jnp.int32)
    in_frame = pair_index < frame_pairs
    in_height = (pair_index >= frame_pairs) & (pair_index < frame_pairs + sixth)
    local_index = jnp.where(in_frame, pair_index, jnp.where(in_height, pair_index - frame_pairs, pair_index - frame_pairs - sixth))
    segment_dims = jnp.where(in_frame, 2 * frame_pairs, 2 * sixth)
    inverse = jnp.power(jnp.float32(10000.0), -2.0 * local_index.astype(jnp.float32) / segment_dims.astype(jnp.float32))
    frame_at = positions // (HGT * WID)
    height_at = positions // WID % HGT
    width_at = positions % WID
    coordinate = jnp.where(in_frame[None, :], frame_at[:, None], jnp.where(in_height[None, :], height_at[:, None], width_at[:, None])).astype(jnp.float32)
    angle_table = coordinate * inverse[None, :]
    cosine = jnp.cos(angle_table)[:, None, :]
    sine_table = jnp.sin(angle_table)[:, None, :]
    paired = tensor.reshape(tensor.shape[0], tensor.shape[1], half_dim, 2)
    even_part = paired[..., 0]
    odd_part = paired[..., 1]
    turned = jnp.stack([even_part * cosine - odd_part * sine_table, even_part * sine_table + odd_part * cosine], axis=-1)
    return turned.reshape(tensor.shape)

def prepare(tensor, gain_vector, positions):
    normed = rms_normed(tensor.astype(jnp.float32), gain_vector)
    head_total = tensor.shape[1] // HEAD_DIM
    turned = rotate_pairs(normed.reshape(tensor.shape[0], head_total, HEAD_DIM), positions)
    return turned.reshape(tensor.shape).astype(jnp.bfloat16)

def gate_vector(timestep, base_slice, weight_slice):
    half_freq = FREQ // 2
    exponent = jnp.arange(half_freq, dtype=jnp.int32).astype(jnp.float32) / half_freq
    frequency = jnp.power(jnp.float32(10000.0), -exponent)
    phase = timestep.astype(jnp.float32)[:, None] * frequency[None, :]
    embedded = jnp.concatenate([jnp.cos(phase), jnp.sin(phase)], axis=1)
    projected = jnp.dot(embedded, weight_slice, precision=lax.Precision.HIGHEST, preferred_element_type=jnp.float32)
    return base_slice + projected[0]

def reference(queries, keys, values, query_gain, key_gain, timestep, gate_base, time_weight):
    positions = jnp.arange(LENGTH, dtype=jnp.int32)
    query_rot = prepare(queries, query_gain, positions).reshape(LENGTH, HEADS, HEAD_DIM)
    key_rot = prepare(keys, key_gain, positions).reshape(LENGTH, HEADS, HEAD_DIM)
    value_heads = values.reshape(LENGTH, HEADS, HEAD_DIM)
    score_scale = 1.0 / math.sqrt(HEAD_DIM)
    block_size = math.gcd(LENGTH, 1024)

    def one_head(head_index):
        head_query = lax.dynamic_index_in_dim(query_rot, head_index, 1, keepdims=False)
        head_key = lax.dynamic_index_in_dim(key_rot, head_index, 1, keepdims=False)
        head_value = lax.dynamic_index_in_dim(value_heads, head_index, 1, keepdims=False)
        query_blocks = head_query.reshape(LENGTH // block_size, block_size, HEAD_DIM)

        def one_block(query_block):
            scores = jnp.dot(query_block, head_key.T, preferred_element_type=jnp.float32) * score_scale
            row_peak = lax.optimization_barrier(jnp.max(scores, axis=1, keepdims=True))
            exponent_values = jnp.exp(scores - row_peak)
            weight_total = lax.optimization_barrier(jnp.sum(exponent_values, axis=1, keepdims=True))
            weights = exponent_values.astype(jnp.bfloat16)
            mixed_out = jnp.dot(weights, head_value, preferred_element_type=jnp.float32)
            return mixed_out / weight_total
        return lax.map(one_block, query_blocks).reshape(LENGTH, HEAD_DIM)
    per_head = lax.map(one_head, jnp.arange(HEADS, dtype=jnp.int32))
    heads_out = jnp.transpose(per_head, (1, 0, 2)).reshape(LENGTH, D)
    gate_full = gate_vector(timestep, gate_base, time_weight)
    return (heads_out * gate_full[None, :]).astype(jnp.bfloat16)
```

```python
import functools
import math

import jax
import jax.numpy as jnp
from jax import lax
from jax.experimental import pallas as pl
from jax.experimental.pallas import tpu as pltpu
from jax.sharding import PartitionSpec as P

HEAD_DIM = 128
FREQ = 256
HGT = 32
WID = 32
EPSILON = 1e-06
CHUNKS = 5
VMEM_LIMIT = 56 * 1024 * 1024


def rotation_tables(positions):
    half_dim = HEAD_DIM // 2
    sixth = HEAD_DIM // 6
    frame_pairs = (HEAD_DIM - 4 * sixth) // 2
    lane = jnp.arange(HEAD_DIM, dtype=jnp.int32)
    pair_index = lane // 2
    in_frame = pair_index < frame_pairs
    in_height = (pair_index >= frame_pairs) & (pair_index < frame_pairs + sixth)
    local_index = jnp.where(
        in_frame,
        pair_index,
        jnp.where(in_height, pair_index - frame_pairs, pair_index - frame_pairs - sixth),
    )
    segment_dims = jnp.where(in_frame, 2 * frame_pairs, 2 * sixth)
    inverse = jnp.power(
        jnp.float32(10000.0),
        -2.0 * local_index.astype(jnp.float32) / segment_dims.astype(jnp.float32),
    )
    frame_at = positions // (HGT * WID)
    height_at = positions // WID % HGT
    width_at = positions % WID
    coordinate = jnp.where(
        in_frame[None, :],
        frame_at[:, None],
        jnp.where(in_height[None, :], height_at[:, None], width_at[:, None]),
    ).astype(jnp.float32)
    angle_table = coordinate * inverse[None, :]
    cosine = jnp.cos(angle_table)
    sine = jnp.sin(angle_table)
    even = (lane % 2 == 0)[None, :]
    return cosine, jnp.where(even, -sine, 0.0), jnp.where(even, 0.0, sine)


def gate_vector(timestep, base_slice, weight_slice):
    half_freq = FREQ // 2
    exponent = jnp.arange(half_freq, dtype=jnp.int32).astype(jnp.float32) / half_freq
    frequency = jnp.power(jnp.float32(10000.0), -exponent)
    phase = timestep.astype(jnp.float32)[:, None] * frequency[None, :]
    embedded = jnp.concatenate([jnp.cos(phase), jnp.sin(phase)], axis=1)
    projected = jnp.dot(
        embedded, weight_slice, precision=lax.Precision.HIGHEST, preferred_element_type=jnp.float32
    )
    return base_slice + projected[0]


def prep_kernel(
    groups, chunks, width, me_ref, q_ref, k_ref, v_ref, qg_ref, kg_ref, c_ref, se_ref, so_ref, *outs
):
    me = me_ref[0]
    total = q_ref.shape[1]
    group_width = total // groups
    cosine, even_sine, odd_sine = c_ref[...], se_ref[...], so_ref[...]

    def inverse_root(ref):
        wide = ref[...].astype(jnp.float32)
        return lax.rsqrt(jnp.mean(wide * wide, axis=-1, keepdims=True) + EPSILON)

    roots = (inverse_root(q_ref), inverse_root(k_ref))
    for relative in range(groups):
        start = lax.rem(me + relative, groups) * group_width
        for chunk in range(chunks):
            out_ref = outs[chunk * groups + relative]
            for part in range(width // HEAD_DIM):
                offset = start + chunk * width + part * HEAD_DIM
                source = pl.ds(pl.multiple_of(offset, HEAD_DIM), HEAD_DIM)
                target = slice(part * HEAD_DIM, (part + 1) * HEAD_DIM)
                for which, (ref, gain_ref) in enumerate(((q_ref, qg_ref), (k_ref, kg_ref))):
                    x = ref[:, source].astype(jnp.float32) * roots[which] * gain_ref[:, source]
                    turned = (
                        x * cosine
                        + pltpu.roll(x, HEAD_DIM - 1, 1) * even_sine
                        + pltpu.roll(x, 1, 1) * odd_sine
                    )
                    out_ref[which, :, target] = turned.astype(jnp.bfloat16)
                out_ref[2, :, target] = v_ref[:, source]


def prepare(me, queries, keys, values, query_gain, key_gain, positions, groups, chunks, width):
    tokens, total = queries.shape
    tile = min(tokens, 64)
    tables = rotation_tables(positions)
    row = pl.BlockSpec((tile, total), lambda i, me: (i, 0))
    gain = pl.BlockSpec((1, total), lambda i, me: (0, 0))
    table = pl.BlockSpec((tile, HEAD_DIM), lambda i, me: (i, 0))
    count = groups * chunks
    return pl.pallas_call(
        functools.partial(prep_kernel, groups, chunks, width),
        grid_spec=pltpu.PrefetchScalarGridSpec(
            num_scalar_prefetch=1,
            grid=(tokens // tile,),
            in_specs=[row, row, row, gain, gain, table, table, table],
            out_specs=[pl.BlockSpec((3, tile, width), lambda i, me: (0, i, 0))] * count,
        ),
        out_shape=[jax.ShapeDtypeStruct((3, tokens, width), jnp.bfloat16)] * count,
        compiler_params=pltpu.CompilerParams(vmem_limit_bytes=VMEM_LIMIT),
        cost_estimate=pl.CostEstimate(
            flops=20 * tokens * total, bytes_accessed=12 * tokens * total, transcendentals=0
        ),
        name="prep",
    )(me, queries, keys, values, query_gain[None, :], key_gain[None, :], *tables)


def attend_kernel(groups, subtiles, blocks, *refs):
    q_refs = refs[:groups]
    k_ref, v_ref, gate_ref = refs[groups : groups + 3]
    out_refs = refs[groups + 3 :]
    rows = q_refs[0].shape[1]
    per_row, per_block = blocks
    factor = math.log2(math.e) / math.sqrt(HEAD_DIM)
    joined = groups // subtiles
    tall = rows * joined
    keys_at = k_ref.shape[3] * per_block

    def query(index):
        return jnp.concatenate([q_refs[index * joined + j][0] for j in range(joined)], axis=0)

    tiles = [query(index) for index in range(subtiles)]

    def advance(step, state):
        outer = step // per_row
        inner = pl.ds(lax.rem(step, per_row) * per_block, per_block)
        key_block = k_ref[outer, inner, 0].reshape(keys_at, HEAD_DIM)
        value_block = v_ref[outer, inner, 0].reshape(keys_at, HEAD_DIM)
        after = []
        for tile, (peak, total, mixed) in zip(tiles, state):
            scores = lax.dot_general(
                tile, key_block, (((1,), (1,)), ((), ())), preferred_element_type=jnp.float32
            )
            new_peak = jnp.maximum(peak, jnp.max(scores, axis=1, keepdims=True))
            shrink = jnp.exp2((peak - new_peak) * factor)
            weights = jnp.exp2((scores - new_peak) * factor)
            total = total * shrink + jnp.sum(weights, axis=1, keepdims=True)
            mixed = mixed * shrink + jnp.dot(
                weights.astype(jnp.bfloat16), value_block, preferred_element_type=jnp.float32
            )
            after.append((new_peak, total, mixed))
        return tuple(after)

    first = (
        jnp.full((tall, 1), -1e30, jnp.float32),
        jnp.zeros((tall, 1), jnp.float32),
        jnp.zeros((tall, HEAD_DIM), jnp.float32),
    )
    state = lax.fori_loop(0, k_ref.shape[0] * per_row, advance, (first,) * subtiles)
    for index, (_, total, mixed) in enumerate(state):
        gated = (mixed / total * gate_ref[...]).astype(jnp.bfloat16)
        for j in range(joined):
            out_refs[index * joined + j][...] = gated[j * rows : (j + 1) * rows]


def attend(pieces, gathered, gate_row):
    groups = len(pieces)
    _, tokens, width = pieces[0].shape
    heads = width // HEAD_DIM
    outer, inner = gathered.shape[0], gathered.shape[1]
    rows = min(tokens, max(16, 1024 // groups))
    per_block = math.gcd(inner, max(1, 1024 // tokens))
    subtiles = math.gcd(groups, 4)
    key_total = outer * inner * tokens
    query_total = groups * tokens
    held = (outer, inner, 1, tokens, HEAD_DIM)
    return pl.pallas_call(
        functools.partial(attend_kernel, groups, subtiles, (inner // per_block, per_block)),
        grid=(heads, tokens // rows),
        in_specs=[pl.BlockSpec((1, rows, HEAD_DIM), lambda h, i: (0, i, h))] * groups
        + [
            pl.BlockSpec(held, lambda h, i: (0, 0, 0, 0, h)),
            pl.BlockSpec(held, lambda h, i: (0, 0, 1, 0, h)),
            pl.BlockSpec((1, HEAD_DIM), lambda h, i: (0, h)),
        ],
        out_specs=[pl.BlockSpec((rows, HEAD_DIM), lambda h, i: (i, h))] * groups,
        out_shape=[jax.ShapeDtypeStruct((tokens, width), jnp.bfloat16)] * groups,
        compiler_params=pltpu.CompilerParams(vmem_limit_bytes=VMEM_LIMIT),
        cost_estimate=pl.CostEstimate(
            flops=4 * query_total * key_total * width,
            bytes_accessed=4 * key_total * width + 4 * query_total * width,
            transcendentals=query_total * key_total * heads,
        ),
        name="attend",
    )(*pieces, gathered, gathered, gate_row)


def place_kernel(groups, chunks, me_ref, *refs):
    out_ref = refs[-1]
    me = me_ref[0]
    group_width = out_ref.shape[1] // groups
    width = refs[0].shape[1]
    for relative in range(groups):
        start = lax.rem(me + relative, groups) * group_width
        for chunk in range(chunks):
            for part in range(width // HEAD_DIM):
                offset = pl.multiple_of(start + chunk * width + part * HEAD_DIM, HEAD_DIM)
                out_ref[:, pl.ds(offset, HEAD_DIM)] = refs[chunk * groups + relative][
                    :, part * HEAD_DIM : (part + 1) * HEAD_DIM
                ]


def place(me, pieces, groups, chunks):
    tokens, width = pieces[0].shape
    total = width * groups * chunks
    tile = min(tokens, 128)
    return pl.pallas_call(
        functools.partial(place_kernel, groups, chunks),
        grid_spec=pltpu.PrefetchScalarGridSpec(
            num_scalar_prefetch=1,
            grid=(tokens // tile,),
            in_specs=[pl.BlockSpec((tile, width), lambda i, me: (i, 0))] * len(pieces),
            out_specs=pl.BlockSpec((tile, total), lambda i, me: (i, 0)),
        ),
        out_shape=jax.ShapeDtypeStruct((tokens, total), jnp.bfloat16),
        compiler_params=pltpu.CompilerParams(vmem_limit_bytes=VMEM_LIMIT),
        cost_estimate=pl.CostEstimate(
            flops=0, bytes_accessed=4 * tokens * total, transcendentals=0
        ),
        name="place",
    )(me, *pieces)


def local(queries, keys, values, query_gain, key_gain, timestep, gate_base, time_weight):
    token_count, width_total = queries.shape
    groups = lax.axis_size("seq")
    fsdp_count = lax.axis_size("fsdp")
    me = lax.axis_index("seq")
    block_index = me * fsdp_count + lax.axis_index("fsdp")
    positions = block_index * token_count + jnp.arange(token_count, dtype=jnp.int32)
    group_width = width_total // groups
    chunks = math.gcd(group_width // HEAD_DIM, CHUNKS)
    width = group_width // chunks
    me_row = me.astype(jnp.int32)[None]

    prepared = prepare(
        me_row, queries, keys, values, query_gain, key_gain, positions, groups, chunks, width
    )
    group_start = me * group_width
    base_slice = lax.dynamic_slice_in_dim(gate_base, group_start, group_width, 0)
    weight_slice = lax.dynamic_slice_in_dim(time_weight, group_start, group_width, 1)
    gate_slice = gate_vector(timestep, base_slice, weight_slice)

    def shifted(array, shift):
        if shift % groups == 0:
            return array
        return lax.ppermute(array, "seq", [(i, (i + shift) % groups) for i in range(groups)])

    arrived = [
        [shifted(prepared[chunk * groups + relative], relative) for relative in range(groups)]
        for chunk in range(chunks)
    ]
    returned = []
    for chunk, pieces in enumerate(arrived):
        own = jnp.stack([piece[1:] for piece in pieces])
        gathered = lax.all_gather(own, "fsdp", axis=0, tiled=False)
        gate_row = gate_slice[None, chunk * width : (chunk + 1) * width]
        outs = attend(pieces, gathered, gate_row)
        returned += [shifted(outs[relative], -relative) for relative in range(groups)]
    return place(me_row, returned, groups, chunks)


def solution(mesh):
    return jax.shard_map(
        local,
        mesh=mesh,
        in_specs=(
            P(("expert", "seq", "fsdp"), None),
            P(("expert", "seq", "fsdp"), None),
            P(("expert", "seq", "fsdp"), None),
            P("expert"),
            P("expert"),
            P("expert"),
            P("expert"),
            P("expert", None),
        ),
        out_specs=P(("expert", "seq", "fsdp"), None),
        check_vma=False,
    )
```

```python
import functools
import math

import jax
import jax.numpy as jnp
from jax import lax
from jax.experimental import pallas as pl
from jax.experimental.pallas import tpu as pltpu
from jax.sharding import PartitionSpec as P

HEAD_DIM = 128
FREQ = 256
HGT = 32
WID = 32
EPSILON = 1e-06
VMEM_LIMIT = 56 * 1024 * 1024


def rotation_tables(positions):
    half_dim = HEAD_DIM // 2
    sixth = HEAD_DIM // 6
    frame_pairs = (HEAD_DIM - 4 * sixth) // 2
    lane = jnp.arange(HEAD_DIM, dtype=jnp.int32)
    pair_index = lane // 2
    in_frame = pair_index < frame_pairs
    in_height = (pair_index >= frame_pairs) & (pair_index < frame_pairs + sixth)
    local_index = jnp.where(
        in_frame,
        pair_index,
        jnp.where(in_height, pair_index - frame_pairs, pair_index - frame_pairs - sixth),
    )
    segment_dims = jnp.where(in_frame, 2 * frame_pairs, 2 * sixth)
    inverse = jnp.power(
        jnp.float32(10000.0),
        -2.0 * local_index.astype(jnp.float32) / segment_dims.astype(jnp.float32),
    )
    frame_at = positions // (HGT * WID)
    height_at = positions // WID % HGT
    width_at = positions % WID
    coordinate = jnp.where(
        in_frame[None, :],
        frame_at[:, None],
        jnp.where(in_height[None, :], height_at[:, None], width_at[:, None]),
    ).astype(jnp.float32)
    angle_table = coordinate * inverse[None, :]
    cosine = jnp.cos(angle_table)
    sine = jnp.sin(angle_table)
    even = (lane % 2 == 0)[None, :]
    return cosine, jnp.where(even, -sine, 0.0), jnp.where(even, 0.0, sine)


def gate_vector(timestep, base_slice, weight_slice):
    half_freq = FREQ // 2
    exponent = jnp.arange(half_freq, dtype=jnp.int32).astype(jnp.float32) / half_freq
    frequency = jnp.power(jnp.float32(10000.0), -exponent)
    phase = timestep.astype(jnp.float32)[:, None] * frequency[None, :]
    embedded = jnp.concatenate([jnp.cos(phase), jnp.sin(phase)], axis=1)
    projected = jnp.dot(
        embedded, weight_slice, precision=lax.Precision.HIGHEST, preferred_element_type=jnp.float32
    )
    return base_slice + projected[0]


def chunk_spans(heads):
    if heads < 4:
        sizes = [1] * heads
    else:
        sizes = [1] + [2] * ((heads - 2) // 2) + [1] * (heads % 2) + [1]
    spans, start = [], 0
    for size in sizes:
        spans.append((start * HEAD_DIM, size * HEAD_DIM))
        start += size
    return spans


def prep_kernel(
    groups, spans, me_ref, q_ref, k_ref, v_ref, qg_ref, kg_ref, c_ref, se_ref, so_ref, *outs
):
    me = me_ref[0]
    total = q_ref.shape[1]
    group_width = total // groups
    cosine, even_sine, odd_sine = c_ref[...], se_ref[...], so_ref[...]

    def inverse_root(ref):
        wide = ref[...].astype(jnp.float32)
        return lax.rsqrt(jnp.mean(wide * wide, axis=-1, keepdims=True) + EPSILON)

    roots = (inverse_root(q_ref), inverse_root(k_ref))
    for relative in range(groups):
        start = lax.rem(me + relative, groups) * group_width
        for chunk, (begin, width) in enumerate(spans):
            out_ref = outs[chunk * groups + relative]
            for part in range(width // HEAD_DIM):
                offset = start + begin + part * HEAD_DIM
                source = pl.ds(pl.multiple_of(offset, HEAD_DIM), HEAD_DIM)
                target = slice(part * HEAD_DIM, (part + 1) * HEAD_DIM)
                for which, (ref, gain_ref) in enumerate(((q_ref, qg_ref), (k_ref, kg_ref))):
                    x = ref[:, source].astype(jnp.float32) * roots[which] * gain_ref[:, source]
                    turned = (
                        x * cosine
                        + pltpu.roll(x, HEAD_DIM - 1, 1) * even_sine
                        + pltpu.roll(x, 1, 1) * odd_sine
                    )
                    out_ref[which, :, target] = turned.astype(jnp.bfloat16)
                out_ref[2, :, target] = v_ref[:, source]


def prepare(me, queries, keys, values, query_gain, key_gain, positions, groups, spans):
    tokens, total = queries.shape
    tile = min(tokens, 64)
    tables = rotation_tables(positions)
    row = pl.BlockSpec((tile, total), lambda i, me: (i, 0))
    gain = pl.BlockSpec((1, total), lambda i, me: (0, 0))
    table = pl.BlockSpec((tile, HEAD_DIM), lambda i, me: (i, 0))
    widths = [width for _, width in spans for _ in range(groups)]
    return pl.pallas_call(
        functools.partial(prep_kernel, groups, spans),
        grid_spec=pltpu.PrefetchScalarGridSpec(
            num_scalar_prefetch=1,
            grid=(tokens // tile,),
            in_specs=[row, row, row, gain, gain, table, table, table],
            out_specs=[pl.BlockSpec((3, tile, width), lambda i, me: (0, i, 0)) for width in widths],
        ),
        out_shape=[jax.ShapeDtypeStruct((3, tokens, width), jnp.bfloat16) for width in widths],
        compiler_params=pltpu.CompilerParams(vmem_limit_bytes=VMEM_LIMIT),
        cost_estimate=pl.CostEstimate(
            flops=20 * tokens * total, bytes_accessed=12 * tokens * total, transcendentals=0
        ),
        name="prep",
    )(me, queries, keys, values, query_gain[None, :], key_gain[None, :], *tables)


def attend_kernel(groups, subtiles, blocks, *refs):
    q_refs = refs[:groups]
    k_ref, v_ref, gate_ref = refs[groups : groups + 3]
    out_refs = refs[groups + 3 :]
    rows = q_refs[0].shape[1]
    per_row, per_block = blocks
    factor = math.log2(math.e) / math.sqrt(HEAD_DIM)
    joined = groups // subtiles
    tall = rows * joined
    keys_at = k_ref.shape[3] * per_block

    def query(index):
        return jnp.concatenate([q_refs[index * joined + j][0] for j in range(joined)], axis=0)

    tiles = [query(index) for index in range(subtiles)]

    def advance(step, state):
        outer = step // per_row
        inner = pl.ds(lax.rem(step, per_row) * per_block, per_block)
        key_block = k_ref[outer, inner, 0].reshape(keys_at, HEAD_DIM)
        value_block = v_ref[outer, inner, 0].reshape(keys_at, HEAD_DIM)
        after = []
        for tile, (peak, total, mixed) in zip(tiles, state):
            scores = lax.dot_general(
                tile, key_block, (((1,), (1,)), ((), ())), preferred_element_type=jnp.float32
            )
            new_peak = jnp.maximum(peak, jnp.max(scores, axis=1, keepdims=True))
            shrink = jnp.exp2((peak - new_peak) * factor)
            weights = jnp.exp2((scores - new_peak) * factor)
            total = total * shrink + jnp.sum(weights, axis=1, keepdims=True)
            mixed = mixed * shrink + jnp.dot(
                weights.astype(jnp.bfloat16), value_block, preferred_element_type=jnp.float32
            )
            after.append((new_peak, total, mixed))
        return tuple(after)

    first = (
        jnp.full((tall, 1), -1e30, jnp.float32),
        jnp.zeros((tall, 1), jnp.float32),
        jnp.zeros((tall, HEAD_DIM), jnp.float32),
    )
    state = lax.fori_loop(0, k_ref.shape[0] * per_row, advance, (first,) * subtiles)
    for index, (_, total, mixed) in enumerate(state):
        gated = (mixed / total * gate_ref[...]).astype(jnp.bfloat16)
        for j in range(joined):
            out_refs[index * joined + j][...] = gated[j * rows : (j + 1) * rows]


def attend(pieces, gathered, gate_row):
    groups = len(pieces)
    _, tokens, width = pieces[0].shape
    heads = width // HEAD_DIM
    outer, inner = gathered.shape[0], gathered.shape[1]
    rows = min(tokens, max(16, 1024 // groups))
    per_block = math.gcd(inner, max(1, 1024 // tokens))
    subtiles = math.gcd(groups, 4)
    key_total = outer * inner * tokens
    query_total = groups * tokens
    held = (outer, inner, 1, tokens, HEAD_DIM)
    return pl.pallas_call(
        functools.partial(attend_kernel, groups, subtiles, (inner // per_block, per_block)),
        grid=(heads, tokens // rows),
        in_specs=[pl.BlockSpec((1, rows, HEAD_DIM), lambda h, i: (0, i, h))] * groups
        + [
            pl.BlockSpec(held, lambda h, i: (0, 0, 0, 0, h)),
            pl.BlockSpec(held, lambda h, i: (0, 0, 1, 0, h)),
            pl.BlockSpec((1, HEAD_DIM), lambda h, i: (0, h)),
        ],
        out_specs=[pl.BlockSpec((rows, HEAD_DIM), lambda h, i: (i, h))] * groups,
        out_shape=[jax.ShapeDtypeStruct((tokens, width), jnp.bfloat16)] * groups,
        compiler_params=pltpu.CompilerParams(vmem_limit_bytes=VMEM_LIMIT),
        cost_estimate=pl.CostEstimate(
            flops=4 * query_total * key_total * width,
            bytes_accessed=4 * key_total * width + 4 * query_total * width,
            transcendentals=query_total * key_total * heads,
        ),
        name="attend",
    )(*pieces, gathered, gathered, gate_row)


def place_kernel(groups, spans, me_ref, *refs):
    out_ref = refs[-1]
    me = me_ref[0]
    group_width = out_ref.shape[1] // groups
    for relative in range(groups):
        start = lax.rem(me + relative, groups) * group_width
        for chunk, (begin, width) in enumerate(spans):
            for part in range(width // HEAD_DIM):
                offset = pl.multiple_of(start + begin + part * HEAD_DIM, HEAD_DIM)
                out_ref[:, pl.ds(offset, HEAD_DIM)] = refs[chunk * groups + relative][
                    :, part * HEAD_DIM : (part + 1) * HEAD_DIM
                ]


def place(me, pieces, groups, spans):
    tokens = pieces[0].shape[0]
    total = sum(piece.shape[1] for piece in pieces)
    tile = min(tokens, 128)
    return pl.pallas_call(
        functools.partial(place_kernel, groups, spans),
        grid_spec=pltpu.PrefetchScalarGridSpec(
            num_scalar_prefetch=1,
            grid=(tokens // tile,),
            in_specs=[
                pl.BlockSpec((tile, piece.shape[1]), lambda i, me: (i, 0)) for piece in pieces
            ],
            out_specs=pl.BlockSpec((tile, total), lambda i, me: (i, 0)),
        ),
        out_shape=jax.ShapeDtypeStruct((tokens, total), jnp.bfloat16),
        compiler_params=pltpu.CompilerParams(vmem_limit_bytes=VMEM_LIMIT),
        cost_estimate=pl.CostEstimate(
            flops=0, bytes_accessed=4 * tokens * total, transcendentals=0
        ),
        name="place",
    )(me, *pieces)


def local(queries, keys, values, query_gain, key_gain, timestep, gate_base, time_weight):
    token_count, width_total = queries.shape
    groups = lax.axis_size("seq")
    fsdp_count = lax.axis_size("fsdp")
    me = lax.axis_index("seq")
    block_index = me * fsdp_count + lax.axis_index("fsdp")
    positions = block_index * token_count + jnp.arange(token_count, dtype=jnp.int32)
    group_width = width_total // groups
    spans = chunk_spans(group_width // HEAD_DIM)
    chunks = len(spans)
    me_row = me.astype(jnp.int32)[None]

    prepared = prepare(
        me_row, queries, keys, values, query_gain, key_gain, positions, groups, spans
    )
    group_start = me * group_width
    base_slice = lax.dynamic_slice_in_dim(gate_base, group_start, group_width, 0)
    weight_slice = lax.dynamic_slice_in_dim(time_weight, group_start, group_width, 1)
    gate_slice = gate_vector(timestep, base_slice, weight_slice)

    def shifted(array, shift):
        if shift % groups == 0:
            return array
        return lax.ppermute(array, "seq", [(i, (i + shift) % groups) for i in range(groups)])

    arrived = [
        [shifted(prepared[chunk * groups + relative], relative) for relative in range(groups)]
        for chunk in range(chunks)
    ]
    def stacked(chunk, after):
        pieces = arrived[chunk]
        if after is not None:
            pieces, _ = lax.optimization_barrier((pieces, after))
        return pieces, jnp.stack([piece[1:] for piece in pieces])

    held = [stacked(0, None)]
    gathers = [lax.all_gather(held[0][1], "fsdp", axis=0, tiled=False)]
    returned, last = [], None
    for chunk, (begin, width) in enumerate(spans):
        gate_row = gate_slice[None, begin : begin + width]
        if chunk + 1 < chunks:
            held.append(stacked(chunk + 1, last))
            gathers.append(lax.all_gather(held[-1][1], "fsdp", axis=0, tiled=False))
            gate_row, _ = lax.optimization_barrier((gate_row, held[-1][1]))
        outs = attend(held[chunk][0], gathers[chunk], gate_row)
        last = outs[0]
        returned += [shifted(outs[relative], -relative) for relative in range(groups)]
    return place(me_row, returned, groups, spans)


def solution(mesh):
    return jax.shard_map(
        local,
        mesh=mesh,
        in_specs=(
            P(("expert", "seq", "fsdp"), None),
            P(("expert", "seq", "fsdp"), None),
            P(("expert", "seq", "fsdp"), None),
            P("expert"),
            P("expert"),
            P("expert"),
            P("expert"),
            P("expert", None),
        ),
        out_specs=P(("expert", "seq", "fsdp"), None),
        check_vma=False,
    )
```
